32 devices in a mesh: leaf: 8 (over y, x, core), loop: 4 (over z).
Axes of the slice: x: 2, y: 2, z: 4, core: 2. Of those that a mesh axis runs over, the one named last changes fastest.
Arguments:
- jacobian_t: bfloat16 [4, 8192, 512], P('loop', 'leaf'), may hold values from -6 to 6
- leaf_block: bfloat16 [4, 8192, 1024], P('loop', 'leaf'), may hold values from -0.1875 to 0.1875
- left_basis: bfloat16 [4, 8192, 128], P('loop', 'leaf'), may hold values from -0.5 to 0.5
- right_basis: bfloat16 [4, 8192, 128], P('loop', 'leaf'), may hold values from -0.1875 to 0.1875
- couplings: bfloat16 [4, 24, 128, 128], P('loop', 'leaf'), may hold values from -0.5 to 0.5
- group_coupling: bfloat16 [4, 16, 128, 128], P('loop', 'leaf'), may hold values from -0.5 to 0.5
- obs_order: int32 [512], replicated, may hold values from 0 to 511, each once
Outputs:
- cross_cov: bfloat16 [4, 8192, 512], P('loop', 'leaf')
- projected: float32 [512, 512], P('leaf')
The draws below stay inside these ranges and needn't reach their ends.
Inputs may be any that keep to these rules, and one draw needn't show every extreme that they name: `obs_order`: each observation 0 to 511 appears exactly once.
All inputs are finite; a program needn't handle non-finite values.
Results may differ from the reference program's by a relative error of at most 0.005.
Values sent between devices are 32-bit elements; how exact they have to be, the bound alone decides.
A program may use at most 64 MiB of HBM per device.

```python
import jax
import jax.numpy as jnp
from jax import lax

LEAF = 1024
RANK = 128
OBS = 512
LEVELS = 3
N_LEAF = 8
N_LOOP = 4


def level_of(own_key, dims, shards, least, largest):
    level, own = 1.0, jax.random.fold_in(own_key, 6)
    for dim, shards_of in shards:
        draws = jnp.exp(jax.random.uniform(jax.random.fold_in(own, dim), (shards_of,), jnp.float32, least / len(shards), largest / len(shards)))
        level = level * jnp.repeat(draws, dims[dim] // shards_of).reshape([-1 if axis == dim else 1 for axis in range(len(dims))])
    return level


def bell_draw(stream_key, shape, deviation, bound, split=(), dtype=jnp.bfloat16):
    values = deviation * jax.random.normal(stream_key, shape, jnp.float32)
    if split:
        values = values * level_of(stream_key, shape, split, -0.22, 0.18)
    return jnp.clip(values, -bound, bound).astype(dtype)


def setup_inputs(seed: int = 0) -> dict:
    seeds = jax.random.split(jax.random.key(seed), 8)
    jacobian_t = bell_draw(seeds[0], (N_LOOP, N_LEAF * LEAF, OBS), 1.0, 6.0, ((0, 4), (1, 8)))
    leaf_block = bell_draw(seeds[1], (N_LOOP, N_LEAF * LEAF, LEAF), LEAF ** -0.5, 0.1875, ((0, 4), (1, 8)))
    left_basis = bell_draw(seeds[2], (N_LOOP, N_LEAF * LEAF, RANK), RANK ** -0.5, 0.5, ((0, 4), (1, 8)))
    right_basis = bell_draw(seeds[3], (N_LOOP, N_LEAF * LEAF, RANK), LEAF ** -0.5, 0.1875, ((0, 4), (1, 8)))
    couplings = bell_draw(seeds[4], (N_LOOP, N_LEAF * LEVELS, RANK, RANK), RANK ** -0.5, 0.5, ((0, 4), (1, 8)))
    group_coupling = bell_draw(seeds[5], (N_LOOP, N_LEAF * 2, RANK, RANK), RANK ** -0.5, 0.5, ((0, 4), (1, 8)))
    obs_order = jax.random.permutation(seeds[6], OBS).astype(jnp.int32)
    return dict(jacobian_t=jacobian_t, leaf_block=leaf_block, left_basis=left_basis, right_basis=right_basis, couplings=couplings, group_coupling=group_coupling, obs_order=obs_order)


def reference(jacobian_t, leaf_block, left_basis, right_basis, couplings, group_coupling, obs_order):
    highest = lax.Precision.HIGHEST
    blocks = jacobian_t.reshape(N_LOOP, N_LEAF, LEAF, OBS)
    lefts = left_basis.reshape(N_LOOP, N_LEAF, LEAF, RANK)
    rights = right_basis.reshape(N_LOOP, N_LEAF, LEAF, RANK)
    dense = leaf_block.reshape(N_LOOP, N_LEAF, LEAF, LEAF)
    coupled = couplings.reshape(N_LOOP, N_LEAF, LEVELS, RANK, RANK).astype(jnp.float32)
    neighbour = group_coupling.reshape(N_LOOP, N_LEAF, 2, RANK, RANK).astype(jnp.float32)

    def group_coef(args):
        basis, field = args
        return jnp.einsum('dlr,dlo->dro', basis.astype(jnp.float32), field.astype(jnp.float32), precision=highest)

    coef = lax.map(group_coef, (rights, blocks))
    mixed = jnp.zeros((N_LOOP, N_LEAF, RANK, OBS), jnp.float32)
    for level in range(LEVELS):
        width = 2 ** level
        sums = coef.reshape(N_LOOP, N_LEAF // width, width, RANK, OBS).sum(axis=2)
        paired = sums.reshape(N_LOOP, N_LEAF // (2 * width), 2, RANK, OBS)[:, :, ::-1]
        paired = paired.reshape(N_LOOP, N_LEAF // width, RANK, OBS)
        sibling = jnp.repeat(paired, width, axis=1)
        mixed = mixed + jnp.einsum('gdrs,gdso->gdro', coupled[:, :, level], sibling, precision=highest)
    total = coef.sum(axis=1)
    before = jnp.roll(total, 1, axis=0)
    after = jnp.roll(total, -1, axis=0)
    mixed = mixed + jnp.einsum('gdrs,gso->gdro', neighbour[:, :, 0], before, precision=highest)
    mixed = mixed + jnp.einsum('gdrs,gso->gdro', neighbour[:, :, 1], after, precision=highest)
    mixed = mixed.astype(jnp.bfloat16)

    def group_out(args):
        block, field, basis, mix = args
        near = jnp.einsum('dlk,dko->dlo', block.astype(jnp.float32), field.astype(jnp.float32), precision=highest)
        far = jnp.einsum('dlr,dro->dlo', basis.astype(jnp.float32), mix.astype(jnp.float32), precision=highest)
        return (near + far).astype(jnp.bfloat16)

    cross = lax.map(group_out, (dense, blocks, lefts, mixed))
    cross_cov = cross.reshape(N_LOOP, N_LEAF * LEAF, OBS)

    def accumulate(carry, args):
        field, result = args
        flat_f = field.reshape(N_LEAF * LEAF, OBS).astype(jnp.float32)
        flat_r = result.reshape(N_LEAF * LEAF, OBS).astype(jnp.float32)
        return carry + jnp.dot(flat_f.T, flat_r, precision=highest), None

    full, unused = lax.scan(accumulate, jnp.zeros((OBS, OBS), jnp.float32), (jacobian_t, cross_cov))
    projected = full[obs_order.astype(jnp.int32)]
    return cross_cov, projected
```

```python
import functools

import jax
import jax.numpy as jnp
from jax import lax
from jax.experimental import pallas as pl
from jax.experimental.pallas import tpu as pltpu
from jax.sharding import PartitionSpec as P

MESH = pl.DeviceIdType.MESH
F32 = jnp.float32
BF16 = jnp.bfloat16


def dot(a, b):
    return jnp.dot(a, b, preferred_element_type=F32)


def split(value):
    high = value.astype(BF16)
    low = (value - high.astype(F32)).astype(BF16)
    return high, low


def stacked(value):
    return jnp.concatenate(split(value), axis=0)


def doubled(value):
    return jnp.concatenate([value, value], axis=1)


def kernel(
    n_leaf, n_loop, x_hbm, l_hbm, u_hbm, v_hbm, c_hbm, g_hbm, order_ref,
    cross_hbm, proj_hbm,
    x_ref, l_ref, u_ref, v_ref, c_ref, xp_ref, m_ref, mb_ref, n_ref, nrecv_ref,
    coef_ref, sums_ref, sib_ref, tot_ref, ends_ref, csend_ref, crecv_ref,
    w_ref, wrecv_ref, mixsend_ref, mixrecv_ref, mixall_ref,
    f_ref, frecv_ref, zs_ref, zr_ref, red_ref, ag_ref, cross_ref, proj_ref,
    load_sem, store_sem, early_send, early_recv, chain_send, chain_recv,
    end_send, end_recv, mix_send, mix_recv, f_send, f_recv, z_send, z_recv,
    ag_send, ag_recv,
):
    levels = n_leaf.bit_length() - 1
    chips = n_leaf // 2
    chip_levels = levels - 1
    pieces, rank, width = sums_ref.shape[1:]
    cells, obs = x_ref.shape
    chip_rows = obs // chips
    z_rows = chip_rows // n_loop
    half_loop = n_loop // 2
    leaf = lax.axis_index("leaf")
    loop = lax.axis_index("loop")
    core = leaf % 2
    chip = leaf // 2
    sibling = leaf + 1 - 2 * core
    owner = loop // half_loop

    def partner(bit):
        mask = 2**bit
        return leaf + mask * (1 - 2 * ((leaf // mask) % 2))

    def tile_of(relative):
        index = 0
        for bit in range(chip_levels):
            step = 2**bit
            index = index + step * (((chip // step) + (relative // step) % 2) % 2)
        return index

    def send(src, dst, send_sem, recv_sem, to_leaf, to_loop):
        copy = pltpu.make_async_remote_copy(
            src_ref=src, dst_ref=dst, send_sem=send_sem, recv_sem=recv_sem,
            device_id={"leaf": to_leaf, "loop": to_loop}, device_id_type=MESH,
        )
        copy.start()
        return copy

    loads = []
    for number, (src, dst) in enumerate((
        (v_hbm.at[0], v_ref), (x_hbm.at[0], x_ref),
        (u_hbm.at[0], u_ref), (c_hbm.at[0], c_ref.at[pl.ds(0, levels)]),
        (g_hbm.at[0], c_ref.at[pl.ds(levels, 2)]), (l_hbm.at[0], l_ref),
    )):
        loads.append(pltpu.make_async_copy(src, dst, load_sem.at[number]))
        loads[-1].start()

    barrier = pltpu.get_barrier_semaphore()
    for bit in range(1, levels):
        pl.semaphore_signal(
            barrier, inc=1, device_id={"leaf": partner(bit), "loop": loop}, device_id_type=MESH
        )
    for offset in range(n_loop):
        there = (loop + offset) % n_loop
        for to_leaf in (leaf, sibling):
            if offset or to_leaf is sibling:
                pl.semaphore_signal(
                    barrier, inc=1, device_id={"leaf": to_leaf, "loop": there}, device_id_type=MESH
                )

    loads[0].wait()
    loads[1].wait()
    coef = lax.dot_general(
        v_ref[...], x_ref[...], (((0,), (0,)), ((), ())), preferred_element_type=F32
    )
    for part in range(2 * pieces):
        coef_ref[part] = coef[:, part * width:(part + 1) * width]
    pl.semaphore_wait(barrier, levels - 1 + 2 * n_loop - 1)
    mine, other = core * pieces, (1 - core) * pieces
    sent = []
    first = []
    for k in range(pieces):
        first.append(send(
            coef_ref.at[other + k], sib_ref.at[k], early_send.at[k], early_recv.at[k],
            sibling, loop,
        ))

    loads[3].wait()
    loads[4].wait()
    csend_ref[...] = c_ref[...].astype(F32)
    copy_c = send(
        csend_ref, crecv_ref, early_send.at[pieces], early_recv.at[pieces], sibling, loop
    )
    chain = {}
    for k in range(pieces):
        first[k].wait_recv()
        tot_ref[0, k] = coef_ref[mine + k] + sib_ref[k]
        chain[1, k] = send(
            tot_ref.at[0, k], sums_ref.at[0, k], chain_send.at[0, k], chain_recv.at[0, k],
            partner(1), loop,
        )

    onehot = (
        lax.broadcasted_iota(jnp.int32, (obs, obs), 0)
        == jnp.broadcast_to(order_ref[...], (obs, obs))
    ).astype(F32).astype(BF16)
    blocks = 4
    step = cells // blocks

    @pl.loop(0, blocks)
    def permute(i):
        rows = pl.ds(pl.multiple_of(i * step, step), step)
        xp_ref[rows, :] = dot(x_ref[rows, :], onehot).astype(BF16)

    loads[2].wait()
    w_ref[...] = lax.dot_general(
        xp_ref[...], u_ref[...], (((0,), (0,)), ((), ())), preferred_element_type=F32
    )
    copy_w = send(
        w_ref, wrecv_ref, early_send.at[pieces + 1], early_recv.at[pieces + 1], sibling, loop
    )
    loads[5].wait()

    def near():
        @pl.loop(0, blocks)
        def multiply(i):
            rows = pl.ds(pl.multiple_of(i * step, step), step)
            value = dot(l_ref[rows, :], x_ref[...])
            m_ref[rows, :] = value
            mb_ref[rows, :] = value.astype(BF16)

    def project():
        high = obs // blocks

        @pl.loop(0, blocks)
        def multiply(i):
            rows = pl.ds(pl.multiple_of(i * high, high), high)
            value = lax.dot_general(
                xp_ref[:, rows], mb_ref[...], (((0,), (0,)), ((), ())),
                preferred_element_type=F32,
            )
            for part in range(2 * pieces):
                n_ref[part, rows, :] = value[:, part * width:(part + 1) * width]

    near()
    for level in range(1, levels):
        for k in range(pieces):
            chain[level, k].wait_recv()
            tot_ref[level, k] = tot_ref[level - 1, k] + sums_ref[level - 1, k]
            if level + 1 < levels:
                chain[level + 1, k] = send(
                    tot_ref.at[level, k], sums_ref.at[level, k],
                    chain_send.at[level, k], chain_recv.at[level, k],
                    partner(level + 1), loop,
                )
            else:
                for way, there in enumerate(((loop + 1) % n_loop, (loop + n_loop - 1) % n_loop)):
                    chain["end", way, k] = send(
                        tot_ref.at[level, k], ends_ref.at[way, k],
                        end_send.at[way, k], end_recv.at[way, k], leaf, there,
                    )
        if level == 1:
            project()
            copy_n = send(
                n_ref.at[pl.ds(other, pieces)], nrecv_ref,
                early_send.at[pieces + 2], early_recv.at[pieces + 2], sibling, loop,
            )

    copy_c.wait_recv()
    copy_w.wait_recv()
    own = [doubled(c_ref[b]) for b in range(levels + 2)]
    theirs = [doubled(crecv_ref[b].astype(BF16)) for b in range(levels + 2)]
    both = [None] + [
        jnp.concatenate([own[b], theirs[b]], axis=0) for b in range(1, levels + 2)
    ]
    w_own, w_own_low = split(w_ref[...])
    w_sib, w_sib_low = split(wrecv_ref[...])
    w_high = jnp.concatenate([w_own, w_sib, w_own_low, w_sib_low], axis=1)
    partial_mix = []
    for k in range(pieces):
        value = jnp.concatenate([
            dot(own[0], stacked(sib_ref[k])),
            dot(theirs[0], stacked(coef_ref[mine + k])),
        ], axis=0)
        for level in range(1, levels):
            value = value + dot(both[level], stacked(sums_ref[level - 1, k]))
        partial_mix.append(value)
    copy_n.wait_recv()
    for k in range(pieces):
        f_ref[k] = (n_ref[mine + k] + nrecv_ref[k]).reshape(chips, chip_rows, width)

    bits = {}
    for k in range(pieces):
        order = list(range(chip_levels))
        bits[k] = order if k % 2 == 0 else order[::-1]

    def stage_tiles(k, stage):
        done = sum(2**bit for bit in bits[k][:stage])
        here = 2**bits[k][stage]
        found = [r for r in range(chips) if not r & done and r & here]
        later = bits[k][stage + 1:]
        found.sort(key=lambda r: [-((r >> bit) & 1) for bit in later])
        return found

    slots = {}
    for k in range(pieces):
        for stage in range(chip_levels):
            for r in stage_tiles(k, stage):
                slots[k, stage, r] = len([key for key in slots if key[0] == k])
    scatter = {}

    def launch(k, stage, r):
        bit = bits[k][stage]
        slot = slots[k, stage, r]
        scatter[k, stage, r] = send(
            f_ref.at[k, tile_of(r)], frecv_ref.at[k, slot],
            f_send.at[k, slot], f_recv.at[k, slot], partner(bit + 1), loop,
        )

    mix_copies = []
    for k in range(pieces):
        value = partial_mix[k]
        for way in range(2):
            chain["end", way, k].wait_recv()
            value = value + dot(both[levels + way], stacked(ends_ref[way, k]))
        rounded = value.astype(BF16)
        mixall_ref[mine + k] = rounded[:rank]
        mixsend_ref[k] = value[rank:]
        far = dot(w_high, jnp.concatenate([rounded, rounded], axis=0))
        f_ref[k] = f_ref[k] + far.reshape(chips, chip_rows, width)
        for r in stage_tiles(k, 0):
            launch(k, 0, r)
        mix_copies.append(send(
            mixsend_ref.at[k], mixrecv_ref.at[k], mix_send.at[k], mix_recv.at[k], sibling, loop
        ))

    for k in range(pieces):
        mix_copies[k].wait_recv()
        mixall_ref[other + k] = mixrecv_ref[k].astype(BF16)
    mix_all = jnp.concatenate([mixall_ref[part] for part in range(2 * pieces)], axis=1)

    @pl.loop(0, blocks)
    def finish(i):
        rows = pl.ds(pl.multiple_of(i * step, step), step)
        cross_ref[rows, :] = (m_ref[rows, :] + dot(u_ref[rows, :], mix_all)).astype(BF16)

    out_cross = pltpu.make_async_copy(cross_ref, cross_hbm.at[0], store_sem.at[0])
    out_cross.start()

    for stage in range(chip_levels):
        for k in range(pieces):
            here = 2**bits[k][stage]
            for r in stage_tiles(k, stage):
                scatter[k, stage, r].wait_recv()
                kept = r ^ here
                tile = tile_of(kept)
                f_ref[k, tile] = f_ref[k, tile] + frecv_ref[k, slots[k, stage, r]]
                if kept:
                    next_stage = stage + 1
                    if kept in stage_tiles(k, next_stage):
                        launch(k, next_stage, kept)

    z_copies = {}
    for k in range(pieces):
        value = f_ref[k, chip]
        for there in range(n_loop):
            zs_ref[k, there] = value[there * z_rows:(there + 1) * z_rows]
        for offset in range(1, n_loop):
            there = (loop + offset) % n_loop
            z_copies[k, offset] = send(
                zs_ref.at[k, there], zr_ref.at[offset - 1, k],
                z_send.at[offset - 1, k], z_recv.at[offset - 1, k], leaf, there,
            )
    for k in range(pieces):
        value = zs_ref[k, loop]
        for offset in range(1, n_loop):
            z_copies[k, offset].wait_recv()
            value = value + zr_ref[offset - 1, k]
        red_ref[k] = value

    place = loop % half_loop
    to_leaf = 2 * chip + owner

    def gather(offset):
        return pltpu.make_async_remote_copy(
            src_ref=red_ref, dst_ref=ag_ref.at[core, place],
            send_sem=ag_send.at[offset], recv_sem=ag_recv.at[core, place],
            device_id={"leaf": to_leaf, "loop": (loop + offset) % n_loop}, device_id_type=MESH,
        )

    for offset in range(1, n_loop):
        gather(offset).start()

    @pl.when(owner != core)
    def across():
        gather(0).start()

    for source in range(2):
        for at in range(half_loop):
            is_own = jnp.logical_and(source == core, core * half_loop + at == loop)

            @pl.when(is_own)
            def keep():
                for k in range(pieces):
                    ag_ref[source, at, k] = red_ref[k]

            @pl.when(jnp.logical_not(is_own))
            def arrive():
                pltpu.make_async_remote_copy(
                    src_ref=red_ref, dst_ref=ag_ref.at[source, at],
                    send_sem=ag_send.at[0], recv_sem=ag_recv.at[source, at],
                    device_id={"leaf": sibling, "loop": loop}, device_id_type=MESH,
                ).wait_recv()

            for k in range(pieces):
                left = (source * pieces + k) * width
                proj_ref[at * z_rows:(at + 1) * z_rows, left:left + width] = ag_ref[source, at, k]

    out_proj = pltpu.make_async_copy(proj_ref, proj_hbm, store_sem.at[1])
    out_proj.start()

    for copy in first + [copy_c, copy_w, copy_n] + mix_copies:
        copy.wait_send()
    for group in (chain, scatter, z_copies):
        for copy in group.values():
            copy.wait_send()
    for offset in range(1, n_loop):
        gather(offset).wait_send()

    @pl.when(owner != core)
    def drain():
        gather(0).wait_send()

    out_cross.wait()
    out_proj.wait()


def solution(mesh):
    n_leaf, n_loop = mesh.shape["leaf"], mesh.shape["loop"]
    levels = n_leaf.bit_length() - 1
    chips = n_leaf // 2

    def body(jacobian_t, leaf_block, left_basis, right_basis, couplings, group_coupling, obs_order):
        _, cells, obs = jacobian_t.shape
        rank = left_basis.shape[-1]
        width = 128
        pieces = obs // 2 // width
        chip_rows = obs // chips
        z_rows = chip_rows // n_loop
        half_loop = n_loop // 2
        anywhere = pl.BlockSpec(memory_space=pl.ANY)
        vmem = pltpu.VMEM
        dma = pltpu.SemaphoreType.DMA
        links = max(levels - 1, 1)
        return tuple(pl.pallas_call(
            functools.partial(kernel, n_leaf, n_loop),
            out_shape=(
                jax.ShapeDtypeStruct((1, cells, obs), BF16),
                jax.ShapeDtypeStruct((obs // n_leaf, obs), F32),
            ),
            in_specs=[anywhere] * 6 + [pl.BlockSpec(memory_space=pltpu.VMEM)],
            out_specs=(anywhere, anywhere),
            scratch_shapes=[
                vmem((cells, obs), BF16),
                vmem((cells, cells), BF16),
                vmem((cells, rank), BF16),
                vmem((cells, rank), BF16),
                vmem((levels + 2, rank, rank), BF16),
                vmem((cells, obs), BF16),
                vmem((cells, obs), F32),
                vmem((cells, obs), BF16),
                vmem((2 * pieces, obs, width), F32),
                vmem((pieces, obs, width), F32),
                vmem((2 * pieces, rank, width), F32),
                vmem((links, pieces, rank, width), F32),
                vmem((pieces, rank, width), F32),
                vmem((levels, pieces, rank, width), F32),
                vmem((2, pieces, rank, width), F32),
                vmem((levels + 2, rank, rank), F32),
                vmem((levels + 2, rank, rank), F32),
                vmem((obs, rank), F32),
                vmem((obs, rank), F32),
                vmem((pieces, rank, width), F32),
                vmem((pieces, rank, width), F32),
                vmem((2 * pieces, rank, width), BF16),
                vmem((pieces, chips, chip_rows, width), F32),
                vmem((pieces, chips, chip_rows, width), F32),
                vmem((pieces, n_loop, z_rows, width), F32),
                vmem((n_loop - 1, pieces, z_rows, width), F32),
                vmem((pieces, z_rows, width), F32),
                vmem((2, half_loop, pieces, z_rows, width), F32),
                vmem((cells, obs), BF16),
                vmem((obs // n_leaf, obs), F32),
                dma((6,)),
                dma((2,)),
                dma((pieces + 3,)),
                dma((pieces + 3,)),
                dma((links, pieces)),
                dma((links, pieces)),
                dma((2, pieces)),
                dma((2, pieces)),
                dma((pieces,)),
                dma((pieces,)),
                dma((pieces, chips)),
                dma((pieces, chips)),
                dma((n_loop - 1, pieces)),
                dma((n_loop - 1, pieces)),
                dma((n_loop,)),
                dma((2, half_loop)),
            ],
            compiler_params=pltpu.CompilerParams(
                collective_id=0, has_side_effects=True, vmem_limit_bytes=60 * 2**20,
            ),
        )(jacobian_t, leaf_block, left_basis, right_basis, couplings, group_coupling,
          obs_order.reshape(1, obs)))

    in_specs = (
        P("loop", "leaf", None),
        P("loop", "leaf", None),
        P("loop", "leaf", None),
        P("loop", "leaf", None),
        P("loop", "leaf", None, None),
        P("loop", "leaf", None, None),
        P(),
    )
    out_specs = (P("loop", "leaf", None), P("leaf", None))
    return jax.shard_map(body, mesh=mesh, in_specs=in_specs, out_specs=out_specs, check_vma=False)
```

```python
import functools

import jax
import jax.numpy as jnp
from jax import lax
from jax.experimental import pallas as pl
from jax.experimental.pallas import tpu as pltpu
from jax.sharding import PartitionSpec as P

MESH = pl.DeviceIdType.MESH
F32 = jnp.float32
BF16 = jnp.bfloat16


def dot(a, b):
    return jnp.dot(a, b, preferred_element_type=F32)


def split(value):
    high = value.astype(BF16)
    low = (value - high.astype(F32)).astype(BF16)
    return high, low


def stacked(value):
    return jnp.concatenate(split(value), axis=0)


def doubled(value):
    return jnp.concatenate([value, value], axis=1)


def kernel(
    n_leaf, n_loop, halves, x_hbm, l_hbm, u_hbm, v_hbm, c_hbm, g_hbm, order_ref,
    cross_hbm, proj_hbm,
    x_ref, l_ref, u_ref, v_ref, c_ref, xp_ref, m_ref, mb_ref, n_ref, nrecv_ref,
    coef_ref, sums_ref, sib_ref, tot_ref, ends_ref, csend_ref, crecv_ref,
    w_ref, wrecv_ref, mixsend_ref, mixrecv_ref, mixall_ref,
    f_ref, frecv_ref, zs_ref, zr_ref, red_ref, ag_ref, cross_ref, proj_ref,
    load_sem, store_sem, early_send, early_recv, chain_send, chain_recv,
    end_send, end_recv, mix_send, mix_recv, f_send, f_recv, z_send, z_recv,
    ag_send, ag_recv, wcat_ref, part_ref, qs_ref, qz_ref, qt_ref, q_send, q_recv,
):
    levels = n_leaf.bit_length() - 1
    chips = n_leaf // 2
    chip_levels = levels - 1
    pieces, rank, width = sums_ref.shape[1:]
    cells, obs = x_ref.shape
    chip_rows = obs // chips
    z_rows = chip_rows // n_loop
    half_loop = n_loop // 2
    leaf = lax.axis_index("leaf")
    loop = lax.axis_index("loop")
    core = leaf % 2
    chip = leaf // 2
    sibling = leaf + 1 - 2 * core
    owner = loop // half_loop

    def partner(bit):
        mask = 2**bit
        return leaf + mask * (1 - 2 * ((leaf // mask) % 2))

    def tile_of(relative):
        index = 0
        for bit in range(chip_levels):
            step = 2**bit
            index = index + step * (((chip // step) + (relative // step) % 2) % 2)
        return index

    def send(src, dst, send_sem, recv_sem, to_leaf, to_loop):
        copy = pltpu.make_async_remote_copy(
            src_ref=src, dst_ref=dst, send_sem=send_sem, recv_sem=recv_sem,
            device_id={"leaf": to_leaf, "loop": to_loop}, device_id_type=MESH,
        )
        copy.start()
        return copy

    loads = []
    for number, (src, dst) in enumerate((
        (v_hbm.at[0], v_ref), (x_hbm.at[0], x_ref),
        (u_hbm.at[0], u_ref), (c_hbm.at[0], c_ref.at[pl.ds(0, levels)]),
        (g_hbm.at[0], c_ref.at[pl.ds(levels, 2)]), (l_hbm.at[0], l_ref),
    )):
        loads.append(pltpu.make_async_copy(src, dst, load_sem.at[number]))
        loads[-1].start()

    barrier = pltpu.get_barrier_semaphore()
    for bit in range(1, levels):
        pl.semaphore_signal(
            barrier, inc=1, device_id={"leaf": partner(bit), "loop": loop}, device_id_type=MESH
        )
    for offset in range(n_loop):
        there = (loop + offset) % n_loop
        for to_leaf in (leaf, sibling):
            if offset or to_leaf is sibling:
                pl.semaphore_signal(
                    barrier, inc=1, device_id={"leaf": to_leaf, "loop": there}, device_id_type=MESH
                )

    loads[0].wait()
    loads[1].wait()
    coef = lax.dot_general(
        v_ref[...], x_ref[...], (((0,), (0,)), ((), ())), preferred_element_type=F32
    )
    for part in range(2 * pieces):
        coef_ref[part] = coef[:, part * width:(part + 1) * width]
    pl.semaphore_wait(barrier, levels - 1 + 2 * n_loop - 1)
    mine, other = core * pieces, (1 - core) * pieces
    sent = []
    first = []
    for k in range(pieces):
        first.append(send(
            coef_ref.at[other + k], sib_ref.at[k], early_send.at[k], early_recv.at[k],
            sibling, loop,
        ))

    loads[3].wait()
    loads[4].wait()
    csend_ref[...] = c_ref[...].astype(F32)
    copy_c = send(
        csend_ref, crecv_ref, early_send.at[pieces], early_recv.at[pieces], sibling, loop
    )
    chain = {}
    high = rank // halves

    def rows_of(half):
        return pl.ds(half * high, high)

    def advance(level, k, half):
        rows = rows_of(half)
        if level + 1 < levels:
            chain[level + 1, k, half] = send(
                tot_ref.at[level, k, rows], sums_ref.at[level, k, rows],
                chain_send.at[level, k, half], chain_recv.at[level, k, half],
                partner(level + 1), loop,
            )
            return
        for way, there in enumerate(((loop + 1) % n_loop, (loop + n_loop - 1) % n_loop)):
            chain["end", way, k, half] = send(
                tot_ref.at[level, k, rows], ends_ref.at[way, k, rows],
                end_send.at[way, k, half], end_recv.at[way, k, half], leaf, there,
            )

    for k in range(pieces):
        first[k].wait_recv()
        tot_ref[0, k] = coef_ref[mine + k] + sib_ref[k]
        for half in range(halves):
            advance(0, k, half)

    onehot = (
        lax.broadcasted_iota(jnp.int32, (obs, obs), 0)
        == jnp.broadcast_to(order_ref[...], (obs, obs))
    ).astype(F32).astype(BF16)
    blocks = 4
    step = cells // blocks

    @pl.loop(0, blocks)
    def permute(i):
        rows = pl.ds(pl.multiple_of(i * step, step), step)
        xp_ref[rows, :] = dot(x_ref[rows, :], onehot).astype(BF16)

    loads[2].wait()
    w_ref[...] = lax.dot_general(
        xp_ref[...], u_ref[...], (((0,), (0,)), ((), ())), preferred_element_type=F32
    )
    copy_w = send(
        w_ref, wrecv_ref, early_send.at[pieces + 1], early_recv.at[pieces + 1], sibling, loop
    )

    bits = {}
    for k in range(pieces + 1):
        order = list(range(chip_levels))
        bits[k] = order if k % 2 == 0 else order[::-1]

    def stage_tiles(k, stage):
        done = sum(2**bit for bit in bits[k][:stage])
        here = 2**bits[k][stage]
        found = [r for r in range(chips) if not r & done and r & here]
        later = bits[k][stage + 1:]
        found.sort(key=lambda r: [-((r >> bit) & 1) for bit in later])
        return found

    slots = {}
    for k in range(pieces + 1):
        for stage in range(chip_levels):
            for r in stage_tiles(k, stage):
                slots[k, stage, r] = len([key for key in slots if key[0] == k])
    scatter = {}

    def launch(k, stage, r):
        bit = bits[k][stage]
        slot = slots[k, stage, r]
        scatter[k, stage, r] = send(
            f_ref.at[k, tile_of(r)], frecv_ref.at[k, slot],
            f_send.at[k, slot], f_recv.at[k, slot], partner(bit + 1), loop,
        )

    def collect(k, stage):
        here = 2**bits[k][stage]
        for r in stage_tiles(k, stage):
            scatter[k, stage, r].wait_recv()
            kept = r ^ here
            tile = tile_of(kept)
            f_ref[k, tile] = f_ref[k, tile] + frecv_ref[k, slots[k, stage, r]]
            if kept and kept in stage_tiles(k, stage + 1):
                launch(k, stage + 1, kept)

    def near():
        @pl.loop(0, blocks)
        def multiply(i):
            rows = pl.ds(pl.multiple_of(i * step, step), step)
            value = dot(l_ref[rows, :], x_ref[...])
            m_ref[rows, :] = value
            mb_ref[rows, :] = value.astype(BF16)

    def project():
        tall = obs // blocks

        @pl.loop(0, blocks)
        def multiply(i):
            rows = pl.ds(pl.multiple_of(i * tall, tall), tall)
            value = lax.dot_general(
                xp_ref[:, rows], mb_ref[...], (((0,), (0,)), ((), ())),
                preferred_element_type=F32,
            )
            for part in range(2 * pieces):
                n_ref[part, rows, :] = value[:, part * width:(part + 1) * width]

    extra = pieces
    for level in range(1, levels):
        for k in range(pieces):
            for half in range(halves):
                rows = rows_of(half)
                chain[level, k, half].wait_recv()
                tot_ref[level, k, rows] = tot_ref[level - 1, k, rows] + sums_ref[level - 1, k, rows]
                advance(level, k, half)
        if level == 1:
            copy_c.wait_recv()
            copy_w.wait_recv()
            w_own, w_own_low = split(w_ref[...])
            w_sib, w_sib_low = split(wrecv_ref[...])
            w_high = jnp.concatenate([w_own, w_sib, w_own_low, w_sib_low], axis=1)
            wcat_ref[...] = w_high
            g_own, g_sib = c_ref[levels + core], crecv_ref[levels + core].astype(BF16)
            reach = dot(w_high, jnp.concatenate([g_own, g_sib, g_own, g_sib], axis=0))
            f_ref[extra] = reach.reshape(chips, chip_rows, width)
            for r in stage_tiles(extra, 0):
                launch(extra, 0, r)
            loads[5].wait()
            near()
            project()
            copy_n = send(
                n_ref.at[pl.ds(other, pieces)], nrecv_ref,
                early_send.at[pieces + 2], early_recv.at[pieces + 2], sibling, loop,
            )

    own = [doubled(c_ref[b]) for b in range(levels)]
    theirs = [doubled(crecv_ref[b].astype(BF16)) for b in range(levels)]
    for k in range(pieces):
        value = jnp.concatenate([
            dot(own[0], stacked(sib_ref[k])),
            dot(theirs[0], stacked(coef_ref[mine + k])),
        ], axis=0)
        for level in range(1, levels):
            both = jnp.concatenate([own[level], theirs[level]], axis=0)
            value = value + dot(both, stacked(sums_ref[level - 1, k]))
        part_ref[k] = value
        rounded = value.astype(BF16)
        far = dot(wcat_ref[...], jnp.concatenate([rounded, rounded], axis=0))
        if k == 0:
            copy_n.wait_recv()
        f_ref[k] = (n_ref[mine + k] + nrecv_ref[k] + far).reshape(chips, chip_rows, width)
        for r in stage_tiles(k, 0):
            launch(k, 0, r)

    for stage in range(chip_levels):
        collect(extra, stage)
    qs_ref[...] = f_ref[extra, chip]
    copy_q = send(
        qs_ref, qz_ref, q_send.at[0], q_recv.at[0],
        leaf, (loop + n_loop - 1 + 2 * core) % n_loop,
    )
    for stage in range(chip_levels - 1):
        for k in range(pieces):
            collect(k, stage)
    copy_q.wait_recv()
    copy_t = send(qz_ref, qt_ref, q_send.at[1], q_recv.at[1], sibling, loop)
    copy_t.wait_recv()
    a_high, a_low = split(qz_ref[...] + qt_ref[...])
    a_all = jnp.concatenate([a_high, a_low, a_high], axis=1)

    z_copies = {}
    for k in range(pieces):
        t_high, t_low = split(tot_ref[levels - 1, k])
        reached = dot(a_all, jnp.concatenate([t_high, t_high, t_low], axis=0))
        if chip_levels:
            collect(k, chip_levels - 1)
        value = f_ref[k, chip] + reached
        for there in range(n_loop):
            zs_ref[k, there] = value[there * z_rows:(there + 1) * z_rows]
        for offset in range(1, n_loop):
            there = (loop + offset) % n_loop
            z_copies[k, offset] = send(
                zs_ref.at[k, there], zr_ref.at[offset - 1, k],
                z_send.at[offset - 1, k], z_recv.at[offset - 1, k], leaf, there,
            )

    mix_copies = []
    for k in range(pieces):
        value = part_ref[k]
        for way in range(2):
            for half in range(halves):
                chain["end", way, k, half].wait_recv()
            both = jnp.concatenate([
                doubled(c_ref[levels + way]), doubled(crecv_ref[levels + way].astype(BF16)),
            ], axis=0)
            value = value + dot(both, stacked(ends_ref[way, k]))
        mixall_ref[mine + k] = value[:rank].astype(BF16)
        mixsend_ref[k] = value[rank:]
        mix_copies.append(send(
            mixsend_ref.at[k], mixrecv_ref.at[k], mix_send.at[k], mix_recv.at[k], sibling, loop
        ))

    place = loop % half_loop
    to_leaf = 2 * chip + owner

    def gather(offset, k):
        return pltpu.make_async_remote_copy(
            src_ref=red_ref.at[k], dst_ref=ag_ref.at[core, place, k],
            send_sem=ag_send.at[offset, k], recv_sem=ag_recv.at[core, place, k],
            device_id={"leaf": to_leaf, "loop": (loop + offset) % n_loop}, device_id_type=MESH,
        )

    for k in range(pieces):
        value = zs_ref[k, loop]
        for offset in range(1, n_loop):
            z_copies[k, offset].wait_recv()
            value = value + zr_ref[offset - 1, k]
        red_ref[k] = value
        for offset in range(1, n_loop):
            gather(offset, k).start()

        @pl.when(owner != core)
        def across():
            gather(0, k).start()

    for k in range(pieces):
        mix_copies[k].wait_recv()
        mixall_ref[other + k] = mixrecv_ref[k].astype(BF16)
    mix_all = jnp.concatenate([mixall_ref[part] for part in range(2 * pieces)], axis=1)

    @pl.loop(0, blocks)
    def finish(i):
        rows = pl.ds(pl.multiple_of(i * step, step), step)
        cross_ref[rows, :] = (m_ref[rows, :] + dot(u_ref[rows, :], mix_all)).astype(BF16)

    out_cross = pltpu.make_async_copy(cross_ref, cross_hbm.at[0], store_sem.at[0])
    out_cross.start()

    for k in range(pieces):
        for source in range(2):
            for at in range(half_loop):
                is_own = jnp.logical_and(source == core, core * half_loop + at == loop)

                @pl.when(is_own)
                def keep():
                    ag_ref[source, at, k] = red_ref[k]

                @pl.when(jnp.logical_not(is_own))
                def arrive():
                    pltpu.make_async_remote_copy(
                        src_ref=red_ref.at[k], dst_ref=ag_ref.at[source, at, k],
                        send_sem=ag_send.at[0, k], recv_sem=ag_recv.at[source, at, k],
                        device_id={"leaf": sibling, "loop": loop}, device_id_type=MESH,
                    ).wait_recv()

                left = (source * pieces + k) * width
                proj_ref[at * z_rows:(at + 1) * z_rows, left:left + width] = ag_ref[source, at, k]

    out_proj = pltpu.make_async_copy(proj_ref, proj_hbm, store_sem.at[1])
    out_proj.start()

    for copy in first + [copy_c, copy_w, copy_n, copy_q, copy_t] + mix_copies:
        copy.wait_send()
    for group in (chain, scatter, z_copies):
        for copy in group.values():
            copy.wait_send()
    for k in range(pieces):
        for offset in range(1, n_loop):
            gather(offset, k).wait_send()

        @pl.when(owner != core)
        def drain():
            gather(0, k).wait_send()

    out_cross.wait()
    out_proj.wait()


def solution(mesh):
    n_leaf, n_loop = mesh.shape["leaf"], mesh.shape["loop"]
    levels = n_leaf.bit_length() - 1
    chips = n_leaf // 2

    def body(jacobian_t, leaf_block, left_basis, right_basis, couplings, group_coupling, obs_order):
        _, cells, obs = jacobian_t.shape
        rank = left_basis.shape[-1]
        width = 128
        pieces = obs // 2 // width
        chip_rows = obs // chips
        z_rows = chip_rows // n_loop
        half_loop = n_loop // 2
        halves = 2
        anywhere = pl.BlockSpec(memory_space=pl.ANY)
        vmem = pltpu.VMEM
        dma = pltpu.SemaphoreType.DMA
        links = max(levels - 1, 1)
        return tuple(pl.pallas_call(
            functools.partial(kernel, n_leaf, n_loop, halves),
            out_shape=(
                jax.ShapeDtypeStruct((1, cells, obs), BF16),
                jax.ShapeDtypeStruct((obs // n_leaf, obs), F32),
            ),
            in_specs=[anywhere] * 6 + [pl.BlockSpec(memory_space=pltpu.VMEM)],
            out_specs=(anywhere, anywhere),
            scratch_shapes=[
                vmem((cells, obs), BF16),
                vmem((cells, cells), BF16),
                vmem((cells, rank), BF16),
                vmem((cells, rank), BF16),
                vmem((levels + 2, rank, rank), BF16),
                vmem((cells, obs), BF16),
                vmem((cells, obs), F32),
                vmem((cells, obs), BF16),
                vmem((2 * pieces, obs, width), F32),
                vmem((pieces, obs, width), F32),
                vmem((2 * pieces, rank, width), F32),
                vmem((links, pieces, rank, width), F32),
                vmem((pieces, rank, width), F32),
                vmem((levels, pieces, rank, width), F32),
                vmem((2, pieces, rank, width), F32),
                vmem((levels + 2, rank, rank), F32),
                vmem((levels + 2, rank, rank), F32),
                vmem((obs, rank), F32),
                vmem((obs, rank), F32),
                vmem((pieces, rank, width), F32),
                vmem((pieces, rank, width), F32),
                vmem((2 * pieces, rank, width), BF16),
                vmem((pieces + 1, chips, chip_rows, width), F32),
                vmem((pieces + 1, chips, chip_rows, width), F32),
                vmem((pieces, n_loop, z_rows, width), F32),
                vmem((n_loop - 1, pieces, z_rows, width), F32),
                vmem((pieces, z_rows, width), F32),
                vmem((2, half_loop, pieces, z_rows, width), F32),
                vmem((cells, obs), BF16),
                vmem((obs // n_leaf, obs), F32),
                dma((6,)),
                dma((2,)),
                dma((pieces + 3,)),
                dma((pieces + 3,)),
                dma((links, pieces, halves)),
                dma((links, pieces, halves)),
                dma((2, pieces, halves)),
                dma((2, pieces, halves)),
                dma((pieces,)),
                dma((pieces,)),
                dma((pieces + 1, chips)),
                dma((pieces + 1, chips)),
                dma((n_loop - 1, pieces)),
                dma((n_loop - 1, pieces)),
                dma((n_loop, pieces)),
                dma((2, half_loop, pieces)),
                vmem((obs, 4 * rank), BF16),
                vmem((pieces, 2 * rank, width), F32),
                vmem((chip_rows, width), F32),
                vmem((chip_rows, width), F32),
                vmem((chip_rows, width), F32),
                dma((2,)),
                dma((2,)),
            ],
            compiler_params=pltpu.CompilerParams(
                collective_id=0, has_side_effects=True, vmem_limit_bytes=60 * 2**20,
            ),
        )(jacobian_t, leaf_block, left_basis, right_basis, couplings, group_coupling,
          obs_order.reshape(1, obs)))

    in_specs = (
        P("loop", "leaf", None),
        P("loop", "leaf", None),
        P("loop", "leaf", None),
        P("loop", "leaf", None),
        P("loop", "leaf", None, None),
        P("loop", "leaf", None, None),
        P(),
    )
    out_specs = (P("loop", "leaf", None), P("leaf", None))
    return jax.shard_map(body, mesh=mesh, in_specs=in_specs, out_specs=out_specs, check_vma=False)
```

```python
import functools

import jax
import jax.numpy as jnp
from jax import lax
from jax.experimental import pallas as pl
from jax.experimental.pallas import tpu as pltpu
from jax.sharding import PartitionSpec as P

MESH = pl.DeviceIdType.MESH
F32 = jnp.float32
BF16 = jnp.bfloat16


def dot(a, b):
    return jnp.dot(a, b, preferred_element_type=F32)


def split(value):
    high = value.astype(BF16)
    low = (value - high.astype(F32)).astype(BF16)
    return high, low


def stacked(value):
    return jnp.concatenate(split(value), axis=0)


def doubled(value):
    return jnp.concatenate([value, value], axis=1)


def kernel(
    n_leaf, n_loop, halves, x_hbm, l_hbm, u_hbm, v_hbm, c_hbm, g_hbm, order_ref,
    cross_hbm, proj_hbm,
    x_ref, l_ref, u_ref, v_ref, c_ref, xp_ref, m_ref, mb_ref, n_ref, nrecv_ref,
    coef_ref, sums_ref, sib_ref, tot_ref, ends_ref, csend_ref, crecv_ref,
    w_ref, wrecv_ref, mixsend_ref, mixrecv_ref, mixall_ref,
    f_ref, frecv_ref, zs_ref, zr_ref, red_ref, ag_ref, cross_ref, proj_ref,
    load_sem, store_sem, early_send, early_recv, chain_send, chain_recv,
    end_send, end_recv, mix_send, mix_recv, f_send, f_recv, z_send, z_recv,
    ag_send, ag_recv, wcat_ref, part_ref, qs_ref, qz_ref, q_send, q_recv,
):
    levels = n_leaf.bit_length() - 1
    chips = n_leaf // 2
    chip_levels = levels - 1
    pieces, rank, width = sums_ref.shape[1:]
    cells, obs = x_ref.shape
    chip_rows = obs // chips
    z_rows = chip_rows // n_loop
    half_loop = n_loop // 2
    leaf = lax.axis_index("leaf")
    loop = lax.axis_index("loop")
    core = leaf % 2
    chip = leaf // 2
    sibling = leaf + 1 - 2 * core
    owner = loop // half_loop

    def partner(bit):
        mask = 2**bit
        return leaf + mask * (1 - 2 * ((leaf // mask) % 2))

    def tile_of(relative):
        index = 0
        for bit in range(chip_levels):
            step = 2**bit
            index = index + step * (((chip // step) + (relative // step) % 2) % 2)
        return index

    def send(src, dst, send_sem, recv_sem, to_leaf, to_loop):
        copy = pltpu.make_async_remote_copy(
            src_ref=src, dst_ref=dst, send_sem=send_sem, recv_sem=recv_sem,
            device_id={"leaf": to_leaf, "loop": to_loop}, device_id_type=MESH,
        )
        copy.start()
        return copy

    loads = []
    for number, (src, dst) in enumerate((
        (v_hbm.at[0], v_ref), (x_hbm.at[0], x_ref),
        (u_hbm.at[0], u_ref), (c_hbm.at[0], c_ref.at[pl.ds(0, levels)]),
        (g_hbm.at[0], c_ref.at[pl.ds(levels, 2)]), (l_hbm.at[0], l_ref),
    )):
        loads.append(pltpu.make_async_copy(src, dst, load_sem.at[number]))
        loads[-1].start()

    barrier = pltpu.get_barrier_semaphore()
    for bit in range(1, levels):
        pl.semaphore_signal(
            barrier, inc=1, device_id={"leaf": partner(bit), "loop": loop}, device_id_type=MESH
        )
    for offset in range(n_loop):
        there = (loop + offset) % n_loop
        for to_leaf in (leaf, sibling):
            if offset or to_leaf is sibling:
                pl.semaphore_signal(
                    barrier, inc=1, device_id={"leaf": to_leaf, "loop": there}, device_id_type=MESH
                )

    loads[0].wait()
    loads[1].wait()
    coef = lax.dot_general(
        v_ref[...], x_ref[...], (((0,), (0,)), ((), ())), preferred_element_type=F32
    )
    for part in range(2 * pieces):
        coef_ref[part] = coef[:, part * width:(part + 1) * width]
    pl.semaphore_wait(barrier, levels - 1 + 2 * n_loop - 1)
    mine, other = core * pieces, (1 - core) * pieces
    sent = []
    first = []
    for k in range(pieces):
        first.append(send(
            coef_ref.at[other + k], sib_ref.at[k], early_send.at[k], early_recv.at[k],
            sibling, loop,
        ))

    loads[3].wait()
    loads[4].wait()
    csend_ref[...] = c_ref[...].astype(F32)
    copy_c = send(
        csend_ref, crecv_ref, early_send.at[pieces], early_recv.at[pieces], sibling, loop
    )
    chain = {}
    high = rank // halves

    def rows_of(half):
        return pl.ds(half * high, high)

    def advance(level, k, half):
        rows = rows_of(half)
        if level + 1 < levels:
            chain[level + 1, k, half] = send(
                tot_ref.at[level, k, rows], sums_ref.at[level, k, rows],
                chain_send.at[level, k, half], chain_recv.at[level, k, half],
                partner(level + 1), loop,
            )
            return
        for way, there in enumerate(((loop + 1) % n_loop, (loop + n_loop - 1) % n_loop)):
            chain["end", way, k, half] = send(
                tot_ref.at[level, k, rows], ends_ref.at[way, k, rows],
                end_send.at[way, k, half], end_recv.at[way, k, half], leaf, there,
            )

    onehot = (
        lax.broadcasted_iota(jnp.int32, (obs, obs), 0)
        == jnp.broadcast_to(order_ref[...], (obs, obs))
    ).astype(F32).astype(BF16)
    blocks = 4
    step = cells // blocks

    @pl.loop(0, blocks)
    def permute(i):
        rows = pl.ds(pl.multiple_of(i * step, step), step)
        xp_ref[rows, :] = dot(x_ref[rows, :], onehot).astype(BF16)

    for k in range(pieces):
        first[k].wait_recv()
        tot_ref[0, k] = coef_ref[mine + k] + sib_ref[k]
        for half in range(halves):
            advance(0, k, half)

    loads[2].wait()
    w_ref[...] = lax.dot_general(
        xp_ref[...], u_ref[...], (((0,), (0,)), ((), ())), preferred_element_type=F32
    )
    copy_w = send(
        w_ref, wrecv_ref, early_send.at[pieces + 1], early_recv.at[pieces + 1], sibling, loop
    )

    bits = {}
    for k in range(pieces + 1):
        order = list(range(chip_levels))
        bits[k] = order if k % 2 == 0 else order[::-1]

    def stage_tiles(k, stage):
        done = sum(2**bit for bit in bits[k][:stage])
        here = 2**bits[k][stage]
        found = [r for r in range(chips) if not r & done and r & here]
        later = bits[k][stage + 1:]
        found.sort(key=lambda r: [-((r >> bit) & 1) for bit in later])
        return found

    slots = {}
    for k in range(pieces + 1):
        for stage in range(chip_levels):
            for r in stage_tiles(k, stage):
                slots[k, stage, r] = len([key for key in slots if key[0] == k])
    scatter = {}

    def launch(k, stage, r):
        bit = bits[k][stage]
        slot = slots[k, stage, r]
        scatter[k, stage, r] = send(
            f_ref.at[k, tile_of(r)], frecv_ref.at[k, slot],
            f_send.at[k, slot], f_recv.at[k, slot], partner(bit + 1), loop,
        )

    def collect(k, stage):
        here = 2**bits[k][stage]
        for r in stage_tiles(k, stage):
            scatter[k, stage, r].wait_recv()
            kept = r ^ here
            tile = tile_of(kept)
            f_ref[k, tile] = f_ref[k, tile] + frecv_ref[k, slots[k, stage, r]]
            if kept and kept in stage_tiles(k, stage + 1):
                launch(k, stage + 1, kept)

    loads[5].wait()
    tall = obs // blocks

    def near(i):
        rows = pl.ds(i * step, step)
        value = dot(l_ref[rows, :], x_ref[...])
        m_ref[rows, :] = value
        mb_ref[rows, :] = value.astype(BF16)

    def project(i):
        rows = pl.ds(i * tall, tall)
        value = lax.dot_general(
            xp_ref[:, rows], mb_ref[...], (((0,), (0,)), ((), ())), preferred_element_type=F32
        )
        for part in range(2 * pieces):
            n_ref[part, rows, :] = value[:, part * width:(part + 1) * width]

    jobs = [functools.partial(near, i) for i in range(blocks)]
    jobs += [functools.partial(project, i) for i in range(blocks)]

    def work(count):
        for job in jobs[:count]:
            job()
        del jobs[:count]

    work(2)
    copy_c.wait_recv()
    copy_w.wait_recv()
    w_own, w_own_low = split(w_ref[...])
    w_sib, w_sib_low = split(wrecv_ref[...])
    w_high = jnp.concatenate([w_own, w_sib, w_own_low, w_sib_low], axis=1)
    wcat_ref[...] = w_high
    g_own, g_sib = c_ref[levels + core], crecv_ref[levels + core].astype(BF16)
    reach = dot(w_high, jnp.concatenate([g_own, g_sib, g_own, g_sib], axis=0))
    f_ref[pieces] = reach.reshape(chips, chip_rows, width)
    for r in stage_tiles(pieces, 0):
        launch(pieces, 0, r)

    extra = pieces
    for level in range(1, levels):
        for k in range(pieces):
            for half in range(halves):
                rows = rows_of(half)
                chain[level, k, half].wait_recv()
                tot_ref[level, k, rows] = tot_ref[level - 1, k, rows] + sums_ref[level - 1, k, rows]
                if level + 1 < levels:
                    advance(level, k, half)
                work(1)
        work(len(jobs))
        if level == 1:
            copy_n = send(
                n_ref.at[pl.ds(other, pieces)], nrecv_ref,
                early_send.at[pieces + 2], early_recv.at[pieces + 2], sibling, loop,
            )

    if chip_levels > 1:
        collect(extra, 0)
    own = [doubled(c_ref[b]) for b in range(levels)]
    theirs = [doubled(crecv_ref[b].astype(BF16)) for b in range(levels)]
    for k in range(pieces):
        value = jnp.concatenate([
            dot(own[0], stacked(sib_ref[k])),
            dot(theirs[0], stacked(coef_ref[mine + k])),
        ], axis=0)
        for level in range(1, levels):
            both = jnp.concatenate([own[level], theirs[level]], axis=0)
            value = value + dot(both, stacked(sums_ref[level - 1, k]))
        part_ref[k] = value
        rounded = value.astype(BF16)
        far = dot(wcat_ref[...], jnp.concatenate([rounded, rounded], axis=0))
        if k == 0:
            copy_n.wait_recv()
        f_ref[k] = (n_ref[mine + k] + nrecv_ref[k] + far).reshape(chips, chip_rows, width)
        for r in stage_tiles(k, 0):
            launch(k, 0, r)

    for stage in range(1 if chip_levels > 1 else 0, chip_levels):
        collect(extra, stage)
    qs_ref[...] = f_ref[extra, chip]
    q_there = (loop + n_loop - 1 + 2 * core) % n_loop
    copy_q = [
        send(qs_ref, qz_ref.at[core], q_send.at[at], q_recv.at[core], to_leaf, q_there)
        for at, to_leaf in enumerate((leaf, sibling))
    ]
    for k in range(pieces):
        for half in range(halves):
            advance(levels - 1, k, half)
    for stage in range(chip_levels - 1):
        for k in range(pieces):
            collect(k, stage)
    for at in range(2):
        pltpu.make_async_remote_copy(
            src_ref=qs_ref, dst_ref=qz_ref.at[at], send_sem=q_send.at[at], recv_sem=q_recv.at[at],
            device_id={"leaf": sibling, "loop": loop}, device_id_type=MESH,
        ).wait_recv()
    a_high, a_low = split(qz_ref[0] + qz_ref[1])
    a_all = jnp.concatenate([a_high, a_low, a_high], axis=1)

    z_copies = {}
    for k in range(pieces):
        t_high, t_low = split(tot_ref[levels - 1, k])
        reached = dot(a_all, jnp.concatenate([t_high, t_high, t_low], axis=0))
        if chip_levels:
            collect(k, chip_levels - 1)
        value = f_ref[k, chip] + reached
        for there in range(n_loop):
            zs_ref[k, there] = value[there * z_rows:(there + 1) * z_rows]
        for offset in range(1, n_loop):
            there = (loop + offset) % n_loop
            z_copies[k, offset] = send(
                zs_ref.at[k, there], zr_ref.at[offset - 1, k],
                z_send.at[offset - 1, k], z_recv.at[offset - 1, k], leaf, there,
            )

    mix_copies = []
    for k in range(pieces):
        value = part_ref[k]
        for way in range(2):
            for half in range(halves):
                chain["end", way, k, half].wait_recv()
            both = jnp.concatenate([
                doubled(c_ref[levels + way]), doubled(crecv_ref[levels + way].astype(BF16)),
            ], axis=0)
            value = value + dot(both, stacked(ends_ref[way, k]))
        mixall_ref[mine + k] = value[:rank].astype(BF16)
        mixsend_ref[k] = value[rank:]
        mix_copies.append(send(
            mixsend_ref.at[k], mixrecv_ref.at[k], mix_send.at[k], mix_recv.at[k], sibling, loop
        ))

    place = loop % half_loop
    to_leaf = 2 * chip + owner

    def gather(offset, k):
        return pltpu.make_async_remote_copy(
            src_ref=red_ref.at[k], dst_ref=ag_ref.at[core, place, k],
            send_sem=ag_send.at[offset, k], recv_sem=ag_recv.at[core, place, k],
            device_id={"leaf": to_leaf, "loop": (loop + offset) % n_loop}, device_id_type=MESH,
        )

    for k in range(pieces):
        value = zs_ref[k, loop]
        for offset in range(1, n_loop):
            z_copies[k, offset].wait_recv()
            value = value + zr_ref[offset - 1, k]
        red_ref[k] = value
        for offset in range(1, n_loop):
            gather(offset, k).start()

        @pl.when(owner != core)
        def across():
            gather(0, k).start()

    for k in range(pieces):
        mix_copies[k].wait_recv()
        mixall_ref[other + k] = mixrecv_ref[k].astype(BF16)
    mix_all = jnp.concatenate([mixall_ref[part] for part in range(2 * pieces)], axis=1)

    @pl.loop(0, blocks)
    def finish(i):
        rows = pl.ds(pl.multiple_of(i * step, step), step)
        cross_ref[rows, :] = (m_ref[rows, :] + dot(u_ref[rows, :], mix_all)).astype(BF16)

    out_cross = pltpu.make_async_copy(cross_ref, cross_hbm.at[0], store_sem.at[0])
    out_cross.start()

    for k in range(pieces):
        for source in range(2):
            for at in range(half_loop):
                is_own = jnp.logical_and(source == core, core * half_loop + at == loop)

                @pl.when(is_own)
                def keep():
                    ag_ref[source, at, k] = red_ref[k]

                @pl.when(jnp.logical_not(is_own))
                def arrive():
                    pltpu.make_async_remote_copy(
                        src_ref=red_ref.at[k], dst_ref=ag_ref.at[source, at, k],
                        send_sem=ag_send.at[0, k], recv_sem=ag_recv.at[source, at, k],
                        device_id={"leaf": sibling, "loop": loop}, device_id_type=MESH,
                    ).wait_recv()

                left = (source * pieces + k) * width
                proj_ref[at * z_rows:(at + 1) * z_rows, left:left + width] = ag_ref[source, at, k]

    out_proj = pltpu.make_async_copy(proj_ref, proj_hbm, store_sem.at[1])
    out_proj.start()

    for copy in first + [copy_c, copy_w, copy_n] + copy_q + mix_copies:
        copy.wait_send()
    for group in (chain, scatter, z_copies):
        for copy in group.values():
            copy.wait_send()
    for k in range(pieces):
        for offset in range(1, n_loop):
            gather(offset, k).wait_send()

        @pl.when(owner != core)
        def drain():
            gather(0, k).wait_send()

    out_cross.wait()
    out_proj.wait()


def solution(mesh):
    n_leaf, n_loop = mesh.shape["leaf"], mesh.shape["loop"]
    levels = n_leaf.bit_length() - 1
    chips = n_leaf // 2

    def body(jacobian_t, leaf_block, left_basis, right_basis, couplings, group_coupling, obs_order):
        _, cells, obs = jacobian_t.shape
        rank = left_basis.shape[-1]
        width = 128
        pieces = obs // 2 // width
        chip_rows = obs // chips
        z_rows = chip_rows // n_loop
        half_loop = n_loop // 2
        halves = 2
        anywhere = pl.BlockSpec(memory_space=pl.ANY)
        vmem = pltpu.VMEM
        dma = pltpu.SemaphoreType.DMA
        links = max(levels - 1, 1)
        return tuple(pl.pallas_call(
            functools.partial(kernel, n_leaf, n_loop, halves),
            out_shape=(
                jax.ShapeDtypeStruct((1, cells, obs), BF16),
                jax.ShapeDtypeStruct((obs // n_leaf, obs), F32),
            ),
            in_specs=[anywhere] * 6 + [pl.BlockSpec(memory_space=pltpu.VMEM)],
            out_specs=(anywhere, anywhere),
            scratch_shapes=[
                vmem((cells, obs), BF16),
                vmem((cells, cells), BF16),
                vmem((cells, rank), BF16),
                vmem((cells, rank), BF16),
                vmem((levels + 2, rank, rank), BF16),
                vmem((cells, obs), BF16),
                vmem((cells, obs), F32),
                vmem((cells, obs), BF16),
                vmem((2 * pieces, obs, width), F32),
                vmem((pieces, obs, width), F32),
                vmem((2 * pieces, rank, width), F32),
                vmem((links, pieces, rank, width), F32),
                vmem((pieces, rank, width), F32),
                vmem((levels, pieces, rank, width), F32),
                vmem((2, pieces, rank, width), F32),
                vmem((levels + 2, rank, rank), F32),
                vmem((levels + 2, rank, rank), F32),
                vmem((obs, rank), F32),
                vmem((obs, rank), F32),
                vmem((pieces, rank, width), F32),
                vmem((pieces, rank, width), F32),
                vmem((2 * pieces, rank, width), BF16),
                vmem((pieces + 1, chips, chip_rows, width), F32),
                vmem((pieces + 1, chips, chip_rows, width), F32),
                vmem((pieces, n_loop, z_rows, width), F32),
                vmem((n_loop - 1, pieces, z_rows, width), F32),
                vmem((pieces, z_rows, width), F32),
                vmem((2, half_loop, pieces, z_rows, width), F32),
                vmem((cells, obs), BF16),
                vmem((obs // n_leaf, obs), F32),
                dma((6,)),
                dma((2,)),
                dma((pieces + 3,)),
                dma((pieces + 3,)),
                dma((links, pieces, halves)),
                dma((links, pieces, halves)),
                dma((2, pieces, halves)),
                dma((2, pieces, halves)),
                dma((pieces,)),
                dma((pieces,)),
                dma((pieces + 1, chips)),
                dma((pieces + 1, chips)),
                dma((n_loop - 1, pieces)),
                dma((n_loop - 1, pieces)),
                dma((n_loop, pieces)),
                dma((2, half_loop, pieces)),
                vmem((obs, 4 * rank), BF16),
                vmem((pieces, 2 * rank, width), F32),
                vmem((chip_rows, width), F32),
                vmem((2, chip_rows, width), F32),
                dma((2,)),
                dma((2,)),
            ],
            compiler_params=pltpu.CompilerParams(
                collective_id=0, has_side_effects=True, vmem_limit_bytes=60 * 2**20,
            ),
        )(jacobian_t, leaf_block, left_basis, right_basis, couplings, group_coupling,
          obs_order.reshape(1, obs)))

    in_specs = (
        P("loop", "leaf", None),
        P("loop", "leaf", None),
        P("loop", "leaf", None),
        P("loop", "leaf", None),
        P("loop", "leaf", None, None),
        P("loop", "leaf", None, None),
        P(),
    )
    out_specs = (P("loop", "leaf", None), P("leaf", None))
    return jax.shard_map(body, mesh=mesh, in_specs=in_specs, out_specs=out_specs, check_vma=False)
```

```python
import functools

import jax
import jax.numpy as jnp
from jax import lax
from jax.experimental import pallas as pl
from jax.experimental.pallas import tpu as pltpu
from jax.sharding import PartitionSpec as P

MESH = pl.DeviceIdType.MESH
F32 = jnp.float32
BF16 = jnp.bfloat16


def dot(a, b):
    return jnp.dot(a, b, preferred_element_type=F32)


def split(value):
    high = value.astype(BF16)
    low = (value - high.astype(F32)).astype(BF16)
    return high, low


def stacked(value):
    return jnp.concatenate(split(value), axis=0)


def doubled(value):
    return jnp.concatenate([value, value], axis=1)


def kernel(
    n_leaf, n_loop, halves, x_hbm, l_hbm, u_hbm, v_hbm, c_hbm, g_hbm, order_ref,
    cross_hbm, proj_ref,
    x_ref, l_ref, u_ref, v_ref, c_ref, xp_ref, m_ref, mb_ref, n_ref, nrecv_ref,
    coef_ref, sums_ref, sib_ref, tot_ref, ends_ref, csend_ref, crecv_ref,
    w_ref, wrecv_ref, mixsend_ref, mixrecv_ref, mixall_ref,
    f_ref, frecv_ref, zs_ref, zr_ref, red_ref, ag_ref, cross_ref,
    load_sem, store_sem, early_send, early_recv, chain_send, chain_recv,
    end_send, end_recv, mix_send, mix_recv, f_send, f_recv, z_send, z_recv,
    ag_send, ag_recv, wcat_ref, part_ref, qs_ref, qz_ref, q_send, q_recv,
):
    levels = n_leaf.bit_length() - 1
    chips = n_leaf // 2
    chip_levels = levels - 1
    pieces, rank, width = sums_ref.shape[1:]
    cells, obs = x_ref.shape
    chip_rows = obs // chips
    z_rows = chip_rows // n_loop
    half_loop = n_loop // 2
    leaf = lax.axis_index("leaf")
    loop = lax.axis_index("loop")
    core = leaf % 2
    chip = leaf // 2
    sibling = leaf + 1 - 2 * core
    owner = loop // half_loop

    def partner(bit):
        mask = 2**bit
        return leaf + mask * (1 - 2 * ((leaf // mask) % 2))

    def tile_of(relative):
        index = 0
        for bit in range(chip_levels):
            step = 2**bit
            index = index + step * (((chip // step) + (relative // step) % 2) % 2)
        return index

    def send(src, dst, send_sem, recv_sem, to_leaf, to_loop):
        copy = pltpu.make_async_remote_copy(
            src_ref=src, dst_ref=dst, send_sem=send_sem, recv_sem=recv_sem,
            device_id={"leaf": to_leaf, "loop": to_loop}, device_id_type=MESH,
        )
        copy.start()
        return copy

    loads = []
    for number, (src, dst) in enumerate((
        (v_hbm.at[0], v_ref), (x_hbm.at[0], x_ref),
        (u_hbm.at[0], u_ref), (c_hbm.at[0], c_ref.at[pl.ds(0, levels)]),
        (g_hbm.at[0], c_ref.at[pl.ds(levels, 2)]), (l_hbm.at[0], l_ref),
    )):
        loads.append(pltpu.make_async_copy(src, dst, load_sem.at[number]))
        loads[-1].start()

    barrier = pltpu.get_barrier_semaphore()
    for bit in range(1, levels):
        pl.semaphore_signal(
            barrier, inc=1, device_id={"leaf": partner(bit), "loop": loop}, device_id_type=MESH
        )
    for offset in range(n_loop):
        there = (loop + offset) % n_loop
        for to_leaf in (leaf, sibling):
            if offset or to_leaf is sibling:
                pl.semaphore_signal(
                    barrier, inc=1, device_id={"leaf": to_leaf, "loop": there}, device_id_type=MESH
                )

    loads[0].wait()
    loads[1].wait()
    coef = lax.dot_general(
        v_ref[...], x_ref[...], (((0,), (0,)), ((), ())), preferred_element_type=F32
    )
    for part in range(2 * pieces):
        coef_ref[part] = coef[:, part * width:(part + 1) * width]
    pl.semaphore_wait(barrier, levels - 1 + 2 * n_loop - 1)
    mine, other = core * pieces, (1 - core) * pieces
    sent = []
    first = []
    for k in range(pieces):
        first.append(send(
            coef_ref.at[other + k], sib_ref.at[k], early_send.at[k], early_recv.at[k],
            sibling, loop,
        ))

    loads[3].wait()
    loads[4].wait()
    csend_ref[...] = c_ref[...].astype(F32)
    copy_c = send(
        csend_ref, crecv_ref, early_send.at[pieces], early_recv.at[pieces], sibling, loop
    )
    chain = {}
    high = rank // halves

    def rows_of(half):
        return pl.ds(half * high, high)

    def advance(level, k, half):
        rows = rows_of(half)
        if level + 1 < levels:
            chain[level + 1, k, half] = send(
                tot_ref.at[level, k, rows], sums_ref.at[level, k, rows],
                chain_send.at[level, k, half], chain_recv.at[level, k, half],
                partner(level + 1), loop,
            )
            return
        for way, there in enumerate(((loop + 1) % n_loop, (loop + n_loop - 1) % n_loop)):
            chain["end", way, k, half] = send(
                tot_ref.at[level, k, rows], ends_ref.at[way, k, rows],
                end_send.at[way, k, half], end_recv.at[way, k, half], leaf, there,
            )

    onehot = (
        lax.broadcasted_iota(jnp.int32, (obs, obs), 0)
        == jnp.broadcast_to(order_ref[...], (obs, obs))
    ).astype(F32).astype(BF16)
    blocks = 4
    step = cells // blocks

    @pl.loop(0, blocks)
    def permute(i):
        rows = pl.ds(pl.multiple_of(i * step, step), step)
        xp_ref[rows, :] = dot(x_ref[rows, :], onehot).astype(BF16)

    for k in range(pieces):
        first[k].wait_recv()
        tot_ref[0, k] = coef_ref[mine + k] + sib_ref[k]
        for half in range(halves):
            advance(0, k, half)

    loads[2].wait()
    w_ref[...] = lax.dot_general(
        xp_ref[...], u_ref[...], (((0,), (0,)), ((), ())), preferred_element_type=F32
    )
    copy_w = send(
        w_ref, wrecv_ref, early_send.at[pieces + 1], early_recv.at[pieces + 1], sibling, loop
    )

    bits = {}
    for k in range(pieces + 1):
        order = list(range(chip_levels))
        bits[k] = order if k % 2 == 0 else order[::-1]

    def stage_tiles(k, stage):
        done = sum(2**bit for bit in bits[k][:stage])
        here = 2**bits[k][stage]
        found = [r for r in range(chips) if not r & done and r & here]
        later = bits[k][stage + 1:]
        found.sort(key=lambda r: [-((r >> bit) & 1) for bit in later])
        return found

    slots = {}
    for k in range(pieces + 1):
        for stage in range(chip_levels):
            for r in stage_tiles(k, stage):
                slots[k, stage, r] = len([key for key in slots if key[0] == k])
    scatter = {}

    def launch(k, stage, r):
        bit = bits[k][stage]
        slot = slots[k, stage, r]
        scatter[k, stage, r] = send(
            f_ref.at[k, tile_of(r)], frecv_ref.at[k, slot],
            f_send.at[k, slot], f_recv.at[k, slot], partner(bit + 1), loop,
        )

    def collect(k, stage):
        here = 2**bits[k][stage]
        for r in stage_tiles(k, stage):
            scatter[k, stage, r].wait_recv()
            kept = r ^ here
            tile = tile_of(kept)
            f_ref[k, tile] = f_ref[k, tile] + frecv_ref[k, slots[k, stage, r]]
            if kept and kept in stage_tiles(k, stage + 1):
                launch(k, stage + 1, kept)

    loads[5].wait()
    tall = obs // blocks

    def near(i):
        rows = pl.ds(i * step, step)
        value = dot(l_ref[rows, :], x_ref[...])
        m_ref[rows, :] = value
        mb_ref[rows, :] = value.astype(BF16)

    def project(i):
        rows = pl.ds(i * tall, tall)
        value = lax.dot_general(
            xp_ref[:, rows], mb_ref[...], (((0,), (0,)), ((), ())), preferred_element_type=F32
        )
        for part in range(2 * pieces):
            n_ref[part, rows, :] = value[:, part * width:(part + 1) * width]

    jobs = [functools.partial(near, i) for i in range(blocks)]
    jobs += [functools.partial(project, i) for i in range(blocks)]

    def work(count):
        for job in jobs[:count]:
            job()
        del jobs[:count]

    work(2)
    copy_c.wait_recv()
    copy_w.wait_recv()
    w_own, w_own_low = split(w_ref[...])
    w_sib, w_sib_low = split(wrecv_ref[...])
    w_high = jnp.concatenate([w_own, w_sib, w_own_low, w_sib_low], axis=1)
    wcat_ref[...] = w_high
    g_own, g_sib = c_ref[levels + core], crecv_ref[levels + core].astype(BF16)
    reach = dot(w_high, jnp.concatenate([g_own, g_sib, g_own, g_sib], axis=0))
    f_ref[pieces] = reach.reshape(chips, chip_rows, width)
    for r in stage_tiles(pieces, 0):
        launch(pieces, 0, r)

    extra = pieces

    def receive(level, k):
        for half in range(halves):
            rows = rows_of(half)
            chain[level, k, half].wait_recv()
            tot_ref[level, k, rows] = tot_ref[level - 1, k, rows] + sums_ref[level - 1, k, rows]
            if level + 1 < levels:
                advance(level, k, half)
            work(1)

    def mixed(level, k):
        both = jnp.concatenate([doubled(c_ref[level]), doubled(crecv_ref[level].astype(BF16))], axis=0)
        return dot(both, stacked(sums_ref[level - 1, k]))

    last = levels - 1
    for level in range(1, last):
        for k in range(pieces):
            receive(level, k)
    work(len(jobs))
    copy_n = send(
        n_ref.at[pl.ds(other, pieces)], nrecv_ref,
        early_send.at[pieces + 2], early_recv.at[pieces + 2], sibling, loop,
    )
    for k in range(pieces):
        value = jnp.concatenate([
            dot(doubled(c_ref[0]), stacked(sib_ref[k])),
            dot(doubled(crecv_ref[0].astype(BF16)), stacked(coef_ref[mine + k])),
        ], axis=0)
        for level in range(1, last):
            value = value + mixed(level, k)
        part_ref[k] = value
    for k in range(pieces):
        if k == pieces - 1 and chip_levels > 1:
            collect(extra, 0)
        receive(last, k)
        value = part_ref[k] + mixed(last, k)
        part_ref[k] = value
        rounded = value.astype(BF16)
        far = dot(wcat_ref[...], jnp.concatenate([rounded, rounded], axis=0))
        if k == 0:
            copy_n.wait_recv()
        f_ref[k] = (n_ref[mine + k] + nrecv_ref[k] + far).reshape(chips, chip_rows, width)
        for r in stage_tiles(k, 0):
            launch(k, 0, r)

    for stage in range(1 if chip_levels > 1 else 0, chip_levels):
        collect(extra, stage)
    qs_ref[...] = f_ref[extra, chip]
    q_there = (loop + n_loop - 1 + 2 * core) % n_loop
    copy_q = [
        send(qs_ref, qz_ref.at[core], q_send.at[at], q_recv.at[core], to_leaf, q_there)
        for at, to_leaf in enumerate((leaf, sibling))
    ]
    for k in range(pieces):
        for half in range(halves):
            advance(levels - 1, k, half)
    for stage in range(chip_levels - 1):
        for k in range(pieces):
            collect(k, stage)
    for at in range(2):
        pltpu.make_async_remote_copy(
            src_ref=qs_ref, dst_ref=qz_ref.at[at], send_sem=q_send.at[at], recv_sem=q_recv.at[at],
            device_id={"leaf": sibling, "loop": loop}, device_id_type=MESH,
        ).wait_recv()
    a_high, a_low = split(qz_ref[0] + qz_ref[1])
    a_all = jnp.concatenate([a_high, a_low, a_high], axis=1)

    z_copies = {}
    for k in range(pieces):
        t_high, t_low = split(tot_ref[levels - 1, k])
        reached = dot(a_all, jnp.concatenate([t_high, t_high, t_low], axis=0))
        if chip_levels:
            collect(k, chip_levels - 1)
        value = f_ref[k, chip] + reached
        for there in range(n_loop):
            zs_ref[k, there] = value[there * z_rows:(there + 1) * z_rows]
        for offset in range(1, n_loop):
            there = (loop + offset) % n_loop
            z_copies[k, offset] = send(
                zs_ref.at[k, there], zr_ref.at[offset - 1, k],
                z_send.at[offset - 1, k], z_recv.at[offset - 1, k], leaf, there,
            )

    mix_copies = []
    for k in range(pieces):
        value = part_ref[k]
        for way in range(2):
            for half in range(halves):
                chain["end", way, k, half].wait_recv()
            both = jnp.concatenate([
                doubled(c_ref[levels + way]), doubled(crecv_ref[levels + way].astype(BF16)),
            ], axis=0)
            value = value + dot(both, stacked(ends_ref[way, k]))
        mixall_ref[mine + k] = value[:rank].astype(BF16)
        mixsend_ref[k] = value[rank:]
        mix_copies.append(send(
            mixsend_ref.at[k], mixrecv_ref.at[k], mix_send.at[k], mix_recv.at[k], sibling, loop
        ))

    place = loop % half_loop
    to_leaf = 2 * chip + owner

    def gather(offset, k):
        return pltpu.make_async_remote_copy(
            src_ref=red_ref.at[k], dst_ref=ag_ref.at[core, place, k],
            send_sem=ag_send.at[offset, k], recv_sem=ag_recv.at[core, place, k],
            device_id={"leaf": to_leaf, "loop": (loop + offset) % n_loop}, device_id_type=MESH,
        )

    for k in range(pieces):
        value = zs_ref[k, loop]
        for offset in range(1, n_loop):
            z_copies[k, offset].wait_recv()
            value = value + zr_ref[offset - 1, k]
        red_ref[k] = value
        for offset in range(1, n_loop):
            gather(offset, k).start()

        @pl.when(owner != core)
        def across():
            gather(0, k).start()

    for k in range(pieces):
        mix_copies[k].wait_recv()
        mixall_ref[other + k] = mixrecv_ref[k].astype(BF16)
    mix_all = jnp.concatenate([mixall_ref[part] for part in range(2 * pieces)], axis=1)

    @pl.loop(0, blocks)
    def finish(i):
        rows = pl.ds(pl.multiple_of(i * step, step), step)
        cross_ref[rows, :] = (m_ref[rows, :] + dot(u_ref[rows, :], mix_all)).astype(BF16)

    out_cross = pltpu.make_async_copy(cross_ref, cross_hbm.at[0], store_sem.at[0])
    out_cross.start()

    for k in range(pieces):
        for source in range(2):
            for at in range(half_loop):
                is_own = jnp.logical_and(source == core, core * half_loop + at == loop)

                @pl.when(is_own)
                def keep():
                    ag_ref[source, at, k] = red_ref[k]

                @pl.when(jnp.logical_not(is_own))
                def arrive():
                    pltpu.make_async_remote_copy(
                        src_ref=red_ref.at[k], dst_ref=ag_ref.at[source, at, k],
                        send_sem=ag_send.at[0, k], recv_sem=ag_recv.at[source, at, k],
                        device_id={"leaf": sibling, "loop": loop}, device_id_type=MESH,
                    ).wait_recv()

                left = (source * pieces + k) * width
                proj_ref[at * z_rows:(at + 1) * z_rows, left:left + width] = ag_ref[source, at, k]


    for copy in first + [copy_c, copy_w, copy_n] + copy_q + mix_copies:
        copy.wait_send()
    for group in (chain, scatter, z_copies):
        for copy in group.values():
            copy.wait_send()
    for k in range(pieces):
        for offset in range(1, n_loop):
            gather(offset, k).wait_send()

        @pl.when(owner != core)
        def drain():
            gather(0, k).wait_send()

    out_cross.wait()


def solution(mesh):
    n_leaf, n_loop = mesh.shape["leaf"], mesh.shape["loop"]
    levels = n_leaf.bit_length() - 1
    chips = n_leaf // 2

    def body(jacobian_t, leaf_block, left_basis, right_basis, couplings, group_coupling, obs_order):
        _, cells, obs = jacobian_t.shape
        rank = left_basis.shape[-1]
        width = 128
        pieces = obs // 2 // width
        chip_rows = obs // chips
        z_rows = chip_rows // n_loop
        half_loop = n_loop // 2
        halves = 2
        anywhere = pl.BlockSpec(memory_space=pl.ANY)
        vmem = pltpu.VMEM
        dma = pltpu.SemaphoreType.DMA
        links = max(levels - 1, 1)
        return tuple(pl.pallas_call(
            functools.partial(kernel, n_leaf, n_loop, halves),
            out_shape=(
                jax.ShapeDtypeStruct((1, cells, obs), BF16),
                jax.ShapeDtypeStruct((obs // n_leaf, obs), F32),
            ),
            in_specs=[anywhere] * 6 + [pl.BlockSpec(memory_space=pltpu.VMEM)],
            out_specs=(anywhere, pl.BlockSpec(memory_space=pltpu.VMEM)),
            scratch_shapes=[
                vmem((cells, obs), BF16),
                vmem((cells, cells), BF16),
                vmem((cells, rank), BF16),
                vmem((cells, rank), BF16),
                vmem((levels + 2, rank, rank), BF16),
                vmem((cells, obs), BF16),
                vmem((cells, obs), F32),
                vmem((cells, obs), BF16),
                vmem((2 * pieces, obs, width), F32),
                vmem((pieces, obs, width), F32),
                vmem((2 * pieces, rank, width), F32),
                vmem((links, pieces, rank, width), F32),
                vmem((pieces, rank, width), F32),
                vmem((levels, pieces, rank, width), F32),
                vmem((2, pieces, rank, width), F32),
                vmem((levels + 2, rank, rank), F32),
                vmem((levels + 2, rank, rank), F32),
                vmem((obs, rank), F32),
                vmem((obs, rank), F32),
                vmem((pieces, rank, width), F32),
                vmem((pieces, rank, width), F32),
                vmem((2 * pieces, rank, width), BF16),
                vmem((pieces + 1, chips, chip_rows, width), F32),
                vmem((pieces + 1, chips, chip_rows, width), F32),
                vmem((pieces, n_loop, z_rows, width), F32),
                vmem((n_loop - 1, pieces, z_rows, width), F32),
                vmem((pieces, z_rows, width), F32),
                vmem((2, half_loop, pieces, z_rows, width), F32),
                vmem((cells, obs), BF16),
                dma((6,)),
                dma((2,)),
                dma((pieces + 3,)),
                dma((pieces + 3,)),
                dma((links, pieces, halves)),
                dma((links, pieces, halves)),
                dma((2, pieces, halves)),
                dma((2, pieces, halves)),
                dma((pieces,)),
                dma((pieces,)),
                dma((pieces + 1, chips)),
                dma((pieces + 1, chips)),
                dma((n_loop - 1, pieces)),
                dma((n_loop - 1, pieces)),
                dma((n_loop, pieces)),
                dma((2, half_loop, pieces)),
                vmem((obs, 4 * rank), BF16),
                vmem((pieces, 2 * rank, width), F32),
                vmem((chip_rows, width), F32),
                vmem((2, chip_rows, width), F32),
                dma((2,)),
                dma((2,)),
            ],
            compiler_params=pltpu.CompilerParams(
                collective_id=0, has_side_effects=True, vmem_limit_bytes=60 * 2**20,
            ),
        )(jacobian_t, leaf_block, left_basis, right_basis, couplings, group_coupling,
          obs_order.reshape(1, obs)))

    in_specs = (
        P("loop", "leaf", None),
        P("loop", "leaf", None),
        P("loop", "leaf", None),
        P("loop", "leaf", None),
        P("loop", "leaf", None, None),
        P("loop", "leaf", None, None),
        P(),
    )
    out_specs = (P("loop", "leaf", None), P("leaf", None))
    return jax.shard_map(body, mesh=mesh, in_specs=in_specs, out_specs=out_specs, check_vma=False)
```
